32 devices in a mesh: op: 8 (over y, x, core), sec: 4 (over z).
Axes of the slice: x: 2, y: 2, z: 4, core: 2. Of those that a mesh axis runs over, the one named last changes fastest.
Arguments:
- psi: bfloat16 [8, 512, 512], P('sec', 'op'), may hold values from -6 to 6
- left_ops: bfloat16 [16, 8, 512, 512], P('op', 'sec'), may hold values from -0.25 to 0.25
- right_ops: bfloat16 [16, 8, 512, 512], P('op', 'sec'), may hold values from -0.0625 to 0.0625
- conn: int32 [16, 8], P('op', 'sec'), may hold values from 0 to 7, as said below
- dims: int32 [8], P('sec'), may hold values from 128 to 512
Outputs:
- sigma: bfloat16 [8, 512, 512], P('sec', 'op')
The draws below stay inside these ranges and needn't reach their ends.
Inputs may be any that keep to these rules, and one draw needn't show every extreme that they name: conn[k, s] lies in the same group of 2 consecutive sectors as s or in the next group, cyclically over the 8 sectors; both occur.
All inputs are finite; a program needn't handle non-finite values.
Results may differ from the reference program's by a relative error of at most 0.0049.
Values may be sent and summed in bfloat16 or wider, within the bound.
A program may use at most 64 MiB of HBM per device.

```python
import jax
import jax.numpy as jnp
from jax import lax

B = 512
K_DEV = 2
S_DEV = 2
K = 16
S = 8
N_OP = 8
N_SEC = 4


def draw_conn(key, part):
    first = jax.random.fold_in(key, 11)
    second = jax.random.fold_in(key, 23)
    count = K_DEV * N_OP
    total = S_DEV * N_SEC
    group = jnp.arange(total, dtype=jnp.int32) // S_DEV
    hop = jax.random.randint(first, (count, total), 0, 2, dtype=jnp.int32)
    slot = jax.random.randint(second, (count, total), 0, S_DEV, dtype=jnp.int32)
    return (group[None, :] + hop) % N_SEC * S_DEV + slot


def with_ends(array, key, low, high):
    shape = array.shape
    place = [jax.random.randint(jax.random.fold_in(key, axis), (), 0, shape[axis]) for axis in range(len(shape))]
    array = array.at[tuple(place)].set(low)
    longest = shape.index(max(shape))
    place[longest] = (place[longest] + 1) % shape[longest]
    return array.at[tuple(place)].set(high)


def steps_of(own_key, shape, shards, least, high):
    def one(dim, shards_of):
        heights = jax.random.uniform(jax.random.fold_in(jax.random.fold_in(own_key, 6), dim), (shards_of,), jnp.float32, least / len(shards), high / len(shards))
        return jnp.repeat(jnp.exp(heights), shape[dim] // shards_of).reshape((-1,) + (1,) * (len(shape) - dim - 1))

    level = one(*shards[0])
    for cut in shards[1:]:
        level = level * one(*cut)
    return level


def gaussian(rng, shape, scale, bound, split=(), kind=jnp.bfloat16):
    entries = jax.random.normal(rng, shape, jnp.float32) * scale
    if len(split) > 0:
        entries = steps_of(rng, shape, split, -0.22, 0.18) * entries
    return jnp.clip(entries, min=-bound, max=bound).astype(kind)


def setup_inputs(seed: int = 0) -> dict:
    arg_keys = jax.random.split(jax.random.key(seed), 6)
    return {
        "psi": gaussian(arg_keys[0], (S, B, B), 1.0, 6.0, ((0, 4), (1, 8))),
        "left_ops": gaussian(arg_keys[1], (K, S, B, B), B ** -0.5, 0.25, ((0, 8), (1, 4))),
        "right_ops": gaussian(arg_keys[2], (K, S, B, B), (B * K_DEV * N_OP) ** -0.5, 0.0625, ((0, 8), (1, 4))),
        "conn": draw_conn(jax.random.fold_in(arg_keys[5], 71), 0),
        "dims": with_ends(jax.random.randint(arg_keys[4], (S,), B // 4, B + 1), jax.random.fold_in(arg_keys[4], 1), B // 4, B).astype(jnp.int32),
    }


def block_mask(dims):
    idx = jnp.arange(B, dtype=jnp.int32)
    keep = (idx[None, :, None] < dims[:, None, None]) & (idx[None, None, :] < dims[:, None, None])
    return keep


def reference(psi, left_ops, right_ops, conn, dims):
    masked = jnp.where(block_mask(dims), psi, jnp.zeros_like(psi))
    targets = jnp.arange(S, dtype=jnp.int32)

    def step(total, items):
        left_s, right_s, psi_s, conn_s = items
        half = jnp.einsum("kij,jm->kim", left_s.astype(jnp.float32), psi_s.astype(jnp.float32), precision=lax.Precision.HIGHEST)
        half = half.astype(jnp.bfloat16)
        term = jnp.einsum("kim,knm->kin", half.astype(jnp.float32), right_s.astype(jnp.float32), precision=lax.Precision.HIGHEST)
        onehot = (conn_s[:, None] == targets[None, :]).astype(jnp.float32)
        total = total + jnp.einsum("kt,kin->tin", onehot, term, precision=lax.Precision.HIGHEST)
        return total, None

    items = (jnp.moveaxis(left_ops, 1, 0), jnp.moveaxis(right_ops, 1, 0), masked, jnp.moveaxis(conn, 1, 0))
    total, _ = lax.scan(step, jnp.zeros((S, B, B), jnp.float32), items)
    total = jnp.where(block_mask(dims), total, jnp.zeros_like(total))
    return total.astype(jnp.bfloat16)
```

```python
import functools

import jax
import jax.numpy as jnp
from jax import lax
from jax.experimental import pallas as pl
from jax.experimental.pallas import tpu as pltpu
from jax.sharding import PartitionSpec as P

MESH = pl.DeviceIdType.MESH


def flip(index, mask, size):
    out, bit = 0, 1
    while bit < size:
        out = out + ((index // bit + mask // bit) % 2) * bit
        bit *= 2
    return out


def kernel(
    n_op, n_sec,
    conn_ref, dims_ref, psi_ref, left_ref, right_ref, out_ref,
    left_v, right_v, got, masked, keep, give, from_core, sums, from_chip, onward, behind,
    load_sem, own_sem, ag_send, ag_recv, fwd_send, fwd_recv,
    core_send, core_recv, chip_send, chip_recv, z_send, z_recv,
):
    kdev, sdev, width, _ = left_ref.shape
    rows = psi_ref.shape[1]
    chips = n_op // 2
    me, sec = lax.axis_index("op"), lax.axis_index("sec")
    core, chip = me % 2, me // 2
    partner = chip * 2 + 1 - core
    after, before = (sec + 1) % n_sec, (sec + n_sec - 1) % n_sec

    def peer_of(j):
        return flip(chip, j, chips) * 2 + core

    loads = [pltpu.make_async_copy(psi_ref, got.at[me], own_sem.at[0])]
    loads[0].start()
    load_l = pltpu.make_async_copy(left_ref, left_v, load_sem.at[0])
    load_r = pltpu.make_async_copy(right_ref, right_v, load_sem.at[1])
    load_l.start()
    load_r.start()

    barrier = pltpu.get_barrier_semaphore()
    friends = [{"op": peer_of(j)} for j in range(1, chips)] + [{"op": partner}, {"sec": after}, {"sec": before}]
    for friend in friends:
        pl.semaphore_signal(barrier, inc=1, device_id=friend, device_id_type=MESH)
    pl.semaphore_wait(barrier, len(friends))

    def remote(src, dst, send, recv, device):
        copy = pltpu.make_async_remote_copy(
            src_ref=src, dst_ref=dst, send_sem=send, recv_sem=recv, device_id=device, device_id_type=MESH
        )
        return copy

    started = []
    gathers = {}
    for j in reversed(range(1, chips)):
        gathers[j] = remote(psi_ref, got.at[me], ag_send.at[j], ag_recv.at[j], {"op": peer_of(j)})
        gathers[j].start()
    shares = {0: remote(psi_ref, got.at[me], fwd_send.at[0], fwd_recv.at[0], {"op": partner})}
    shares[0].start()
    for j in range(1, chips):
        gathers[j].wait_recv()
        peer = peer_of(j)
        shares[j] = remote(got.at[peer], got.at[peer], fwd_send.at[j], fwd_recv.at[j], {"op": partner})
        shares[j].start()
    loads[0].wait()
    for j in range(chips):
        shares[j].wait_recv()
    for d in range(n_op):
        row = d * rows + lax.broadcasted_iota(jnp.int32, (rows, width), 0)
        col = lax.broadcasted_iota(jnp.int32, (rows, width), 1)
        for s in range(sdev):
            inside = (row < dims_ref[s]) & (col < dims_ref[s])
            masked[s, d * rows:(d + 1) * rows, :] = jnp.where(inside, got[d, s], jnp.zeros((), got.dtype))
    load_l.wait()
    load_r.wait()

    weights = {}
    for k in range(kdev):
        for s in range(sdev):
            away = (conn_ref[k, s] // sdev != sec).astype(jnp.int32)
            slot = conn_ref[k, s] % sdev
            for g in range(2):
                for t in range(sdev):
                    hit = ((slot == t) & (away == 1 - g)).astype(jnp.float32)
                    weights[k, s, g, t] = hit

    core_copies, chip_copies = {}, {}

    def compute(j):
        first = pl.multiple_of(flip(chip, j, chips) * (2 * rows), 2 * rows)
        terms = {}
        for s in range(sdev):
            lhs = left_v[:, s, pl.ds(first, 2 * rows), :].reshape(kdev * 2 * rows, width)
            half = jnp.dot(lhs, masked[s], preferred_element_type=jnp.float32).astype(jnp.bfloat16)
            for k in range(kdev):
                terms[k, s] = lax.dot_general(
                    half[k * 2 * rows:(k + 1) * 2 * rows], right_v[k, s],
                    (((1,), (1,)), ((), ())), preferred_element_type=jnp.float32,
                )
        for g in range(2):
            for t in range(sdev):
                total = sum(weights[k, s, g, t] * terms[k, s] for k in range(kdev) for s in range(sdev))
                keep[j, g, t] = total
                give[j, g, t] = total.astype(jnp.bfloat16)
        theirs = pl.multiple_of((1 - core) * rows, rows)
        for g in range(2):
            core_copies[j, g] = remote(
                give.at[j, g, :, pl.ds(theirs, rows), :], from_core.at[j, g],
                core_send.at[j, g], core_recv.at[j, g], {"op": partner},
            )
            core_copies[j, g].start()

    def pair_sum(j, g):
        core_copies[j, g].wait_recv()
        mine = pl.multiple_of(core * rows, rows)
        return keep[j, g, :, pl.ds(mine, rows), :] + from_core[j, g].astype(jnp.float32)

    def pass_on(j):
        for g in range(2):
            sums[j, g] = pair_sum(j, g).astype(jnp.bfloat16)
            chip_copies[j, g] = remote(
                sums.at[j, g], from_chip.at[j, g], chip_send.at[j, g], chip_recv.at[j, g], {"op": peer_of(j)}
            )
            chip_copies[j, g].start()

    for j in reversed(range(chips)):
        compute(j)
        if j + 1 < chips:
            pass_on(j + 1)

    def collect(g):
        total = pair_sum(0, g)
        for j in reversed(range(1, chips)):
            chip_copies[j, g].wait_recv()
            total = total + from_chip[j, g].astype(jnp.float32)
        return total

    onward[...] = collect(0).astype(jnp.bfloat16)
    shift = remote(onward, behind, z_send.at[0], z_recv.at[0], {"sec": after})
    shift.start()
    own = collect(1)
    keep[0, 1, :, 0:rows, :] = own
    shift.wait_recv()
    for s in range(sdev):
        row = me * rows + lax.broadcasted_iota(jnp.int32, (rows, width), 0)
        col = lax.broadcasted_iota(jnp.int32, (rows, width), 1)
        inside = (row < dims_ref[s]) & (col < dims_ref[s])
        value = keep[0, 1, s, 0:rows, :] + behind[s].astype(jnp.float32)
        out_ref[s] = jnp.where(inside, value, jnp.zeros_like(value)).astype(out_ref.dtype)

    for copies in (gathers, shares, core_copies, chip_copies, {0: shift}):
        for copy in copies.values():
            copy.wait_send()


def on_device(n_op, n_sec, psi, left_ops, right_ops, conn, dims):
    sdev, rows, width = psi.shape
    kdev = left_ops.shape[0]
    chips = n_op // 2
    bf16, f32 = jnp.bfloat16, jnp.float32
    dma = pltpu.SemaphoreType.DMA
    smem = pl.BlockSpec(memory_space=pltpu.SMEM)
    hbm = pl.BlockSpec(memory_space=pl.ANY)
    return pl.pallas_call(
        functools.partial(kernel, n_op, n_sec),
        out_shape=jax.ShapeDtypeStruct(psi.shape, psi.dtype),
        in_specs=[smem, smem, hbm, hbm, hbm],
        out_specs=pl.BlockSpec(memory_space=pltpu.VMEM),
        scratch_shapes=[
            pltpu.VMEM(left_ops.shape, bf16),
            pltpu.VMEM(right_ops.shape, bf16),
            pltpu.VMEM((n_op, sdev, rows, width), bf16),
            pltpu.VMEM((sdev, width, width), bf16),
            pltpu.VMEM((chips, 2, sdev, 2 * rows, width), f32),
            pltpu.VMEM((chips, 2, sdev, 2 * rows, width), bf16),
            pltpu.VMEM((chips, 2, sdev, rows, width), bf16),
            pltpu.VMEM((chips, 2, sdev, rows, width), bf16),
            pltpu.VMEM((chips, 2, sdev, rows, width), bf16),
            pltpu.VMEM((sdev, rows, width), bf16),
            pltpu.VMEM((sdev, rows, width), bf16),
            dma((2,)),
            dma((1,)),
            dma((chips,)), dma((chips,)),
            dma((chips,)), dma((chips,)),
            dma((chips, 2)), dma((chips, 2)),
            dma((chips, 2)), dma((chips, 2)),
            dma((1,)), dma((1,)),
        ],
        compiler_params=pltpu.CompilerParams(
            collective_id=0, has_side_effects=True, vmem_limit_bytes=48 * 1024 * 1024
        ),
    )(conn, dims, psi, left_ops, right_ops)


def solution(mesh):
    return jax.shard_map(
        functools.partial(on_device, mesh.shape["op"], mesh.shape["sec"]),
        mesh=mesh,
        in_specs=(
            P("sec", "op", None),
            P("op", "sec", None, None),
            P("op", "sec", None, None),
            P("op", "sec"),
            P("sec"),
        ),
        out_specs=P("sec", "op", None),
        check_vma=False,
    )
```

```python
import functools

import jax
import jax.numpy as jnp
from jax import lax
from jax.experimental import pallas as pl
from jax.experimental.pallas import tpu as pltpu
from jax.sharding import PartitionSpec as P

MESH = pl.DeviceIdType.MESH


def flip(index, mask, size):
    out, bit = 0, 1
    while bit < size:
        out = out + ((index // bit + mask // bit) % 2) * bit
        bit *= 2
    return out


def kernel(
    n_op, n_sec,
    conn_hbm, dims_hbm, psi_ref, left_ref, right_ref, out_ref,
    conn_ref, dims_ref,
    left_v, right_v, got, masked, keep, give, from_core, early, arrived, sums, from_chip, onward, behind,
    load_sem, own_sem, ag_send, ag_recv, fwd_send, fwd_recv,
    core_send, core_recv, ahead_send, ahead_recv, chip_send, chip_recv, z_send, z_recv,
):
    kdev, sdev, width, _ = left_ref.shape
    rows = psi_ref.shape[1]
    chips = n_op // 2
    me, sec = lax.axis_index("op"), lax.axis_index("sec")
    core, chip = me % 2, me // 2
    partner = chip * 2 + 1 - core
    after, before = (sec + 1) % n_sec, (sec + n_sec - 1) % n_sec

    def peer_of(j):
        return flip(chip, j, chips) * 2 + core

    loads = [pltpu.make_async_copy(psi_ref, got.at[me], own_sem.at[0])]
    loads[0].start()
    load_l = pltpu.make_async_copy(left_ref, left_v, load_sem.at[0])
    load_r = pltpu.make_async_copy(right_ref, right_v, load_sem.at[1])
    load_conn = pltpu.make_async_copy(conn_hbm, conn_ref, load_sem.at[2])
    load_dims = pltpu.make_async_copy(dims_hbm, dims_ref, load_sem.at[3])
    load_conn.start()
    load_dims.start()
    load_l.start()
    load_r.start()

    barrier = pltpu.get_barrier_semaphore()
    friends = [{"op": peer_of(j)} for j in range(1, chips)] + [{"op": partner}, {"sec": after}, {"sec": before}]
    for friend in friends:
        pl.semaphore_signal(barrier, inc=1, device_id=friend, device_id_type=MESH)
    pl.semaphore_wait(barrier, len(friends))

    def remote(src, dst, send, recv, device):
        copy = pltpu.make_async_remote_copy(
            src_ref=src, dst_ref=dst, send_sem=send, recv_sem=recv, device_id=device, device_id_type=MESH
        )
        return copy

    half_s, half_r = sdev // 2, rows // 2
    relayed = chips == 4
    order = [1, 2, 3] if relayed else list(range(1, chips))
    sent = []

    def go(copy):
        copy.start()
        sent.append(copy)
        return copy

    def part(r):
        return pl.ds(r * half_s, half_s)

    gathers, shares = {}, {}
    for first in (0, 1):
        for j in order[:2] if relayed else order:
            r = first if j % 2 == 1 else 1 - first
            gathers[j, r] = go(remote(
                psi_ref.at[part(r)], got.at[me, part(r)], ag_send.at[j, r], ag_recv.at[j, r], {"op": peer_of(j)}
            ))
    for r in (0, 1):
        shares[0, r] = go(remote(
            psi_ref.at[part(r)], got.at[me, part(r)], fwd_send.at[0, r], fwd_recv.at[0, r], {"op": partner}
        ))
    if relayed:
        arrivals = [(1, 0), (2, 1), (1, 1), (2, 0), (3, 0), (3, 1)]
    else:
        arrivals = [(j, r) for j in order for r in (0, 1)]

    def forward(j, r):
        gathers[j, r].wait_recv()
        slab = got.at[peer_of(j), part(r)]
        if relayed and (j, r) in ((1, 0), (2, 1)):
            gathers[3, r] = go(remote(slab, slab, ag_send.at[3, r], ag_recv.at[3, r], {"op": peer_of(3 - j)}))
        shares[j, r] = go(remote(slab, slab, fwd_send.at[j, r], fwd_recv.at[j, r], {"op": partner}))

    def mask_in(d):
        row = d * rows + lax.broadcasted_iota(jnp.int32, (rows, width), 0)
        col = lax.broadcasted_iota(jnp.int32, (rows, width), 1)
        for s in range(sdev):
            inside = (row < dims_ref[s]) & (col < dims_ref[s])
            masked[s, pl.ds(pl.multiple_of(d * rows, rows), rows), :] = jnp.where(
                inside, got[d, s], jnp.zeros((), got.dtype)
            )

    def mask_shared(j):
        for r in (0, 1):
            shares[j, r].wait_recv()
        mask_in(flip(chip, j, chips) * 2 + 1 - core)

    for j, r in arrivals[:4]:
        forward(j, r)
    loads[0].wait()
    load_conn.wait()
    load_dims.wait()
    mask_in(me)
    for j in order[:2]:
        mask_in(peer_of(j))
    for j in [0] + order[:2]:
        mask_shared(j)
    for j, r in arrivals[4:]:
        forward(j, r)
    for j in order[2:]:
        mask_in(peer_of(j))
    for j in order[2:]:
        mask_shared(j)
    load_l.wait()
    load_r.wait()

    weights = {}
    for k in range(kdev):
        for s in range(sdev):
            away = (conn_ref[k, s] // sdev != sec).astype(jnp.int32)
            slot = conn_ref[k, s] % sdev
            for g in range(2):
                for t in range(sdev):
                    hit = ((slot == t) & (away == 1 - g)).astype(jnp.float32)
                    weights[k, s, g, t] = hit

    core_copies = {}

    def compute(j):
        first = pl.multiple_of(flip(chip, j, chips) * (2 * rows), 2 * rows)
        terms = {}
        for s in range(sdev):
            lhs = left_v[:, s, pl.ds(first, 2 * rows), :].reshape(kdev * 2 * rows, width)
            half = jnp.dot(lhs, masked[s], preferred_element_type=jnp.float32).astype(jnp.bfloat16)
            for k in range(kdev):
                terms[k, s] = lax.dot_general(
                    half[k * 2 * rows:(k + 1) * 2 * rows], right_v[k, s],
                    (((1,), (1,)), ((), ())), preferred_element_type=jnp.float32,
                )
        theirs = pl.multiple_of((1 - core) * rows, rows)
        for g in range(2):
            for t in range(sdev):
                total = sum(weights[k, s, g, t] * terms[k, s] for k in range(kdev) for s in range(sdev))
                keep[j, g, t] = total
                give[j, g, t] = total.astype(jnp.bfloat16)
        for g in range(2):
            core_copies[j, g] = go(remote(
                give.at[j, g, :, pl.ds(theirs, rows), :], from_core.at[j, g],
                core_send.at[j, g], core_recv.at[j, g], {"op": partner},
            ))

    group_of, slots_of = (0, 1, 1), (1, 1, 0)

    def pair_sum(j, g, r_slot, r=None):
        start, count = (0, rows) if r is None else (r * half_r, half_r)
        mine = pl.multiple_of(core * rows + start, half_r)
        slots = slice(r_slot * half_s, (r_slot + 1) * half_s)
        return keep[j, g, slots, pl.ds(mine, count), :] + from_core[
            j, g, slots, start:start + count, :
        ].astype(jnp.float32)

    ahead, chip_copies = {}, {}

    def send_ahead(j):
        core_copies[j, 0].wait_recv()
        early[j] = pair_sum(j, 0, 0).astype(jnp.bfloat16)
        ahead[j] = go(remote(early.at[j], arrived.at[j], ahead_send.at[j], ahead_recv.at[j], {"sec": after}))

    def is_relay(j):
        return relayed and j == 3

    def needs_relay(j, r):
        return relayed and (j, r) in ((1, 1), (2, 0))

    def send_piece(j, p, r):
        value = pair_sum(j, group_of[p], slots_of[p], r)
        rs = slice(r * half_r, (r + 1) * half_r)
        if p == 2:
            value = value + arrived[j, :, rs, :].astype(jnp.float32)
        if needs_relay(j, r):
            chip_copies[3, p, r].wait_recv()
            value = value + from_chip[3, p, :, rs, :].astype(jnp.float32)
        sums[j, p, :, rs, :] = value.astype(jnp.bfloat16)
        via = (1 if r == 0 else 2) if is_relay(j) else j
        chip_copies[j, p, r] = go(remote(
            sums.at[j, p, :, rs, :], from_chip.at[j, p, :, rs, :],
            chip_send.at[j, p, r], chip_recv.at[j, p, r], {"op": peer_of(via)},
        ))

    def send_now(j, p):
        for r in (0, 1):
            if not needs_relay(j, r):
                send_piece(j, p, r)

    def handle(j):
        send_ahead(j)
        send_now(j, 0)
        core_copies[j, 1].wait_recv()
        send_now(j, 1)

    chunks = list(reversed(order)) + [0]
    for i, j in enumerate(chunks):
        compute(j)
        if i >= 1:
            handle(chunks[i - 1])
    if order:
        ahead[order[-1]].wait_recv()
        send_now(order[-1], 2)
    if relayed:
        for p in (0, 1):
            send_piece(1, p, 1)
            send_piece(2, p, 0)
    send_ahead(0)
    core_copies[0, 1].wait_recv()
    for j in reversed(order[:-1]):
        ahead[j].wait_recv()
        send_now(j, 2)
    if relayed:
        send_piece(1, 2, 1)
        send_piece(2, 2, 0)

    sources = order[:2] if relayed else order

    def collect(p):
        total = pair_sum(0, group_of[p], slots_of[p])
        for j in sources:
            for r in (0, 1):
                chip_copies[j, p, r].wait_recv()
            total = total + from_chip[j, p].astype(jnp.float32)
        return total

    onward[...] = collect(0).astype(jnp.bfloat16)
    shift = go(remote(onward, behind, z_send.at[0], z_recv.at[0], {"sec": after}))

    def put(slot, value):
        row = me * rows + lax.broadcasted_iota(jnp.int32, (rows, width), 0)
        col = lax.broadcasted_iota(jnp.int32, (rows, width), 1)
        for i in range(half_s):
            s = slot * half_s + i
            inside = (row < dims_ref[s]) & (col < dims_ref[s])
            out_ref[s] = jnp.where(inside, value[i], jnp.zeros_like(value[i])).astype(out_ref.dtype)

    own = collect(1)
    ahead[0].wait_recv()
    put(0, collect(2) + arrived[0].astype(jnp.float32))
    shift.wait_recv()
    put(1, own + behind[...].astype(jnp.float32))

    for copy in sent:
        copy.wait_send()


def on_device(n_op, n_sec, psi, left_ops, right_ops, conn, dims):
    sdev, rows, width = psi.shape
    kdev = left_ops.shape[0]
    chips, half = n_op // 2, sdev // 2
    bf16, f32 = jnp.bfloat16, jnp.float32
    dma = pltpu.SemaphoreType.DMA
    hbm = pl.BlockSpec(memory_space=pl.ANY)
    return pl.pallas_call(
        functools.partial(kernel, n_op, n_sec),
        out_shape=jax.ShapeDtypeStruct(psi.shape, psi.dtype),
        in_specs=[hbm] * 5,
        out_specs=pl.BlockSpec(memory_space=pltpu.VMEM),
        scratch_shapes=[
            pltpu.SMEM(conn.shape, conn.dtype),
            pltpu.SMEM(dims.shape, dims.dtype),
            pltpu.VMEM(left_ops.shape, bf16),
            pltpu.VMEM(right_ops.shape, bf16),
            pltpu.VMEM((n_op, sdev, rows, width), bf16),
            pltpu.VMEM((sdev, width, width), bf16),
            pltpu.VMEM((chips, 2, sdev, 2 * rows, width), f32),
            pltpu.VMEM((chips, 2, sdev, 2 * rows, width), bf16),
            pltpu.VMEM((chips, 2, sdev, rows, width), bf16),
            pltpu.VMEM((chips, half, rows, width), bf16),
            pltpu.VMEM((chips, half, rows, width), bf16),
            pltpu.VMEM((chips, 3, half, rows, width), bf16),
            pltpu.VMEM((chips, 3, half, rows, width), bf16),
            pltpu.VMEM((half, rows, width), bf16),
            pltpu.VMEM((half, rows, width), bf16),
            dma((4,)),
            dma((1,)),
            dma((chips, 2)), dma((chips, 2)),
            dma((chips, 2)), dma((chips, 2)),
            dma((chips, 2)), dma((chips, 2)),
            dma((chips,)), dma((chips,)),
            dma((chips, 3, 2)), dma((chips, 3, 2)),
            dma((1,)), dma((1,)),
        ],
        compiler_params=pltpu.CompilerParams(
            collective_id=0, has_side_effects=True, vmem_limit_bytes=60 * 1024 * 1024
        ),
    )(conn, dims, psi, left_ops, right_ops)


def solution(mesh):
    return jax.shard_map(
        functools.partial(on_device, mesh.shape["op"], mesh.shape["sec"]),
        mesh=mesh,
        in_specs=(
            P("sec", "op", None),
            P("op", "sec", None, None),
            P("op", "sec", None, None),
            P("op", "sec"),
            P("sec"),
        ),
        out_specs=P("sec", "op", None),
        check_vma=False,
    )
```

```python
import functools

import jax
import jax.numpy as jnp
from jax import lax
from jax.experimental import pallas as pl
from jax.experimental.pallas import tpu as pltpu
from jax.sharding import PartitionSpec as P

MESH = pl.DeviceIdType.MESH


def flip(index, mask, size):
    out, bit = 0, 1
    while bit < size:
        out = out + ((index // bit + mask // bit) % 2) * bit
        bit *= 2
    return out


def kernel(
    n_op, n_sec,
    conn_hbm, dims_hbm, psi_ref, left_ref, right_ref, out_ref,
    conn_ref, dims_ref,
    left_v, right_v, got, masked, begun, keep, give, from_core, early, arrived, sums, from_chip, onward, behind,
    load_sem, own_sem, ag_send, ag_recv, fwd_send, fwd_recv,
    core_send, core_recv, ahead_send, ahead_recv, chip_send, chip_recv, z_send, z_recv,
):
    kdev, sdev, width, _ = left_ref.shape
    rows = psi_ref.shape[1]
    chips = n_op // 2
    me, sec = lax.axis_index("op"), lax.axis_index("sec")
    core, chip = me % 2, me // 2
    partner = chip * 2 + 1 - core
    after, before = (sec + 1) % n_sec, (sec + n_sec - 1) % n_sec

    def peer_of(j):
        return flip(chip, j, chips) * 2 + core

    loads = [pltpu.make_async_copy(psi_ref, got.at[me], own_sem.at[0])]
    loads[0].start()
    load_l = pltpu.make_async_copy(left_ref, left_v, load_sem.at[0])
    load_r = pltpu.make_async_copy(right_ref, right_v, load_sem.at[1])
    load_conn = pltpu.make_async_copy(conn_hbm, conn_ref, load_sem.at[2])
    load_dims = pltpu.make_async_copy(dims_hbm, dims_ref, load_sem.at[3])
    load_conn.start()
    load_dims.start()
    load_l.start()
    load_r.start()

    barrier = pltpu.get_barrier_semaphore()
    friends = [{"op": peer_of(j)} for j in range(1, chips)] + [{"op": partner}, {"sec": after}, {"sec": before}]
    for friend in friends:
        pl.semaphore_signal(barrier, inc=1, device_id=friend, device_id_type=MESH)
    pl.semaphore_wait(barrier, len(friends))

    def remote(src, dst, send, recv, device):
        copy = pltpu.make_async_remote_copy(
            src_ref=src, dst_ref=dst, send_sem=send, recv_sem=recv, device_id=device, device_id_type=MESH
        )
        return copy

    half_s, half_r = sdev // 2, rows // 2
    relayed = chips == 4
    order = [1, 2, 3] if relayed else list(range(1, chips))
    sent = []

    def go(copy):
        copy.start()
        sent.append(copy)
        return copy

    def part(r):
        return pl.ds(r * half_s, half_s)

    gathers, shares = {}, {}
    for r in (0, 1):
        shares[0, r] = go(remote(
            psi_ref.at[part(r)], got.at[me, part(r)], fwd_send.at[0, r], fwd_recv.at[0, r], {"op": partner}
        ))
    for r in (0, 1):
        for j in reversed(order):
            gathers[j, r] = go(remote(
                psi_ref.at[part(r)], got.at[me, part(r)], ag_send.at[j, r], ag_recv.at[j, r], {"op": peer_of(j)}
            ))

    def mask_in(d, r):
        row = d * rows + lax.broadcasted_iota(jnp.int32, (rows, width), 0)
        col = lax.broadcasted_iota(jnp.int32, (rows, width), 1)
        for s in range(r * half_s, (r + 1) * half_s):
            inside = (row < dims_ref[s]) & (col < dims_ref[s])
            masked[s, pl.ds(pl.multiple_of(d * rows, rows), rows), :] = jnp.where(
                inside, got[d, s], jnp.zeros((), got.dtype)
            )

    def gather(r):
        for j in order:
            gathers[j, r].wait_recv()
            slab = got.at[peer_of(j), part(r)]
            shares[j, r] = go(remote(slab, slab, fwd_send.at[j, r], fwd_recv.at[j, r], {"op": partner}))
        for j in [0] + order:
            mask_in(peer_of(j), r)
        for j in [0] + order:
            shares[j, r].wait_recv()
            mask_in(flip(chip, j, chips) * 2 + 1 - core, r)

    def terms_of(j, s):
        first = pl.multiple_of(flip(chip, j, chips) * (2 * rows), 2 * rows)
        lhs = left_v[:, s, pl.ds(first, 2 * rows), :].reshape(kdev * 2 * rows, width)
        half = jnp.dot(lhs, masked[s], preferred_element_type=jnp.float32).astype(jnp.bfloat16)
        return [lax.dot_general(
            half[k * 2 * rows:(k + 1) * 2 * rows], right_v[k, s],
            (((1,), (1,)), ((), ())), preferred_element_type=jnp.float32,
        ) for k in range(kdev)]

    chunks = list(reversed(order)) + [0]
    loads[0].wait()
    load_conn.wait()
    load_dims.wait()
    gather(0)
    load_l.wait()
    load_r.wait()
    for j in chunks[:2]:
        for s in range(half_s):
            for k, value in enumerate(terms_of(j, s)):
                begun[j, k, s] = value
    gather(1)

    weights = {}
    for k in range(kdev):
        for s in range(sdev):
            away = (conn_ref[k, s] // sdev != sec).astype(jnp.int32)
            slot = conn_ref[k, s] % sdev
            for g in range(2):
                for t in range(sdev):
                    hit = ((slot == t) & (away == 1 - g)).astype(jnp.float32)
                    weights[k, s, g, t] = hit

    core_copies = {}

    def compute(j):
        terms = {}
        for s in range(sdev):
            if s < half_s and j in chunks[:2]:
                values = [begun[j, k, s] for k in range(kdev)]
            else:
                values = terms_of(j, s)
            for k in range(kdev):
                terms[k, s] = values[k]
        theirs = pl.multiple_of((1 - core) * rows, rows)
        for g in range(2):
            for t in range(sdev):
                total = sum(weights[k, s, g, t] * terms[k, s] for k in range(kdev) for s in range(sdev))
                keep[j, g, t] = total
                give[j, g, t] = total.astype(jnp.bfloat16)
            core_copies[j, g] = go(remote(
                give.at[j, g, :, pl.ds(theirs, rows), :], from_core.at[j, g],
                core_send.at[j, g], core_recv.at[j, g], {"op": partner},
            ))

    group_of, slots_of, via_neighbour = (0, 1, 1), (1, 1, 0), (1,)

    def pair_sum(j, g, r_slot, r=None):
        start, count = (0, rows) if r is None else (r * half_r, half_r)
        mine = pl.multiple_of(core * rows + start, half_r)
        slots = slice(r_slot * half_s, (r_slot + 1) * half_s)
        return keep[j, g, slots, pl.ds(mine, count), :] + from_core[
            j, g, slots, start:start + count, :
        ].astype(jnp.float32)

    ahead, chip_copies = {}, {}

    def send_ahead(j):
        core_copies[j, 0].wait_recv()
        early[j] = pair_sum(j, 0, 0).astype(jnp.bfloat16)
        ahead[j] = go(remote(early.at[j], arrived.at[j], ahead_send.at[j], ahead_recv.at[j], {"sec": after}))

    def is_relay(j, p):
        return relayed and p in via_neighbour and j == 3

    def needs_relay(j, p, r):
        return relayed and p in via_neighbour and (j, r) in ((1, 1), (2, 0))

    def send_piece(j, p, r):
        value = pair_sum(j, group_of[p], slots_of[p], r)
        rs = slice(r * half_r, (r + 1) * half_r)
        if p == 2:
            value = value + arrived[j, :, rs, :].astype(jnp.float32)
        if needs_relay(j, p, r):
            chip_copies[3, p, r].wait_recv()
            value = value + from_chip[3, p, :, rs, :].astype(jnp.float32)
        sums[j, p, :, rs, :] = value.astype(jnp.bfloat16)
        via = (1 if r == 0 else 2) if is_relay(j, p) else j
        chip_copies[j, p, r] = go(remote(
            sums.at[j, p, :, rs, :], from_chip.at[j, p, :, rs, :],
            chip_send.at[j, p, r], chip_recv.at[j, p, r], {"op": peer_of(via)},
        ))

    def send_now(j, p):
        for r in (0, 1):
            if not needs_relay(j, p, r):
                send_piece(j, p, r)

    def relays(p):
        if relayed and p in via_neighbour:
            send_piece(1, p, 1)
            send_piece(2, p, 0)

    def own_now(j):
        core_copies[j, 1].wait_recv()
        send_now(j, 1)

    for i, j in enumerate(chunks):
        compute(j)
        if i >= 1:
            send_ahead(chunks[i - 1])
            send_now(chunks[i - 1], 0)
        if i >= 2:
            own_now(chunks[i - 2])
    if order:
        own_now(chunks[-2])
        ahead[chunks[0]].wait_recv()
        send_now(chunks[0], 2)
    send_ahead(0)
    core_copies[0, 1].wait_recv()
    relays(1)

    def sources(p):
        return order[:2] if relayed and p in via_neighbour else order

    def collect(p):
        total = pair_sum(0, group_of[p], slots_of[p])
        for j in sources(p):
            for r in (0, 1):
                chip_copies[j, p, r].wait_recv()
            total = total + from_chip[j, p].astype(jnp.float32)
        return total

    for j in chunks[1:-1]:
        ahead[j].wait_recv()
        send_now(j, 2)
    relays(2)
    onward[...] = collect(0).astype(jnp.bfloat16)
    shift = go(remote(onward, behind, z_send.at[0], z_recv.at[0], {"sec": after}))

    def put(slot, value):
        row = me * rows + lax.broadcasted_iota(jnp.int32, (rows, width), 0)
        col = lax.broadcasted_iota(jnp.int32, (rows, width), 1)
        for i in range(half_s):
            s = slot * half_s + i
            inside = (row < dims_ref[s]) & (col < dims_ref[s])
            out_ref[s] = jnp.where(inside, value[i], jnp.zeros_like(value[i])).astype(out_ref.dtype)

    own = collect(1)
    ahead[0].wait_recv()
    put(0, collect(2) + arrived[0].astype(jnp.float32))
    shift.wait_recv()
    put(1, own + behind[...].astype(jnp.float32))

    for copy in sent:
        copy.wait_send()


def on_device(n_op, n_sec, psi, left_ops, right_ops, conn, dims):
    sdev, rows, width = psi.shape
    kdev = left_ops.shape[0]
    chips, half = n_op // 2, sdev // 2
    bf16, f32 = jnp.bfloat16, jnp.float32
    dma = pltpu.SemaphoreType.DMA
    hbm = pl.BlockSpec(memory_space=pl.ANY)
    return pl.pallas_call(
        functools.partial(kernel, n_op, n_sec),
        out_shape=jax.ShapeDtypeStruct(psi.shape, psi.dtype),
        in_specs=[hbm] * 5,
        out_specs=pl.BlockSpec(memory_space=pltpu.VMEM),
        scratch_shapes=[
            pltpu.SMEM(conn.shape, conn.dtype),
            pltpu.SMEM(dims.shape, dims.dtype),
            pltpu.VMEM(left_ops.shape, bf16),
            pltpu.VMEM(right_ops.shape, bf16),
            pltpu.VMEM((n_op, sdev, rows, width), bf16),
            pltpu.VMEM((sdev, width, width), bf16),
            pltpu.VMEM((chips, kdev, half, 2 * rows, width), f32),
            pltpu.VMEM((chips, 2, sdev, 2 * rows, width), f32),
            pltpu.VMEM((chips, 2, sdev, 2 * rows, width), bf16),
            pltpu.VMEM((chips, 2, sdev, rows, width), bf16),
            pltpu.VMEM((chips, half, rows, width), bf16),
            pltpu.VMEM((chips, half, rows, width), bf16),
            pltpu.VMEM((chips, 3, half, rows, width), bf16),
            pltpu.VMEM((chips, 3, half, rows, width), bf16),
            pltpu.VMEM((half, rows, width), bf16),
            pltpu.VMEM((half, rows, width), bf16),
            dma((4,)),
            dma((1,)),
            dma((chips, 2)), dma((chips, 2)),
            dma((chips, 2)), dma((chips, 2)),
            dma((chips, 2)), dma((chips, 2)),
            dma((chips,)), dma((chips,)),
            dma((chips, 3, 2)), dma((chips, 3, 2)),
            dma((1,)), dma((1,)),
        ],
        compiler_params=pltpu.CompilerParams(
            collective_id=0, has_side_effects=True, vmem_limit_bytes=60 * 1024 * 1024
        ),
    )(conn, dims, psi, left_ops, right_ops)


def solution(mesh):
    return jax.shard_map(
        functools.partial(on_device, mesh.shape["op"], mesh.shape["sec"]),
        mesh=mesh,
        in_specs=(
            P("sec", "op", None),
            P("op", "sec", None, None),
            P("op", "sec", None, None),
            P("op", "sec"),
            P("sec"),
        ),
        out_specs=P("sec", "op", None),
        check_vma=False,
    )
```

```python
import functools

import jax
import jax.numpy as jnp
from jax import lax
from jax.experimental import pallas as pl
from jax.experimental.pallas import tpu as pltpu
from jax.sharding import PartitionSpec as P

MESH = pl.DeviceIdType.MESH


def flip(index, mask, size):
    out, bit = 0, 1
    while bit < size:
        out = out + ((index // bit + mask // bit) % 2) * bit
        bit *= 2
    return out


def kernel(
    n_op, n_sec,
    conn_hbm, dims_hbm, psi_ref, left_ref, right_ref, out_ref,
    conn_ref, dims_ref,
    left_v, right_v, got, masked, begun, keep, give, from_core, early, arrived, sums, from_chip, onward, behind,
    load_sem, own_sem, ag_send, ag_recv, fwd_send, fwd_recv,
    core_send, core_recv, ahead_send, ahead_recv, chip_send, chip_recv, z_send, z_recv,
):
    kdev, sdev, width, _ = left_ref.shape
    rows = psi_ref.shape[1]
    chips = n_op // 2
    me, sec = lax.axis_index("op"), lax.axis_index("sec")
    core, chip = me % 2, me // 2
    partner = chip * 2 + 1 - core
    after, before = (sec + 1) % n_sec, (sec + n_sec - 1) % n_sec

    def peer_of(j):
        return flip(chip, j, chips) * 2 + core

    loads = [pltpu.make_async_copy(psi_ref, got.at[me], own_sem.at[0])]
    loads[0].start()
    load_l = pltpu.make_async_copy(left_ref, left_v, load_sem.at[0])
    load_r = pltpu.make_async_copy(right_ref, right_v, load_sem.at[1])
    load_conn = pltpu.make_async_copy(conn_hbm, conn_ref, load_sem.at[2])
    load_dims = pltpu.make_async_copy(dims_hbm, dims_ref, load_sem.at[3])
    load_conn.start()
    load_dims.start()
    load_l.start()
    load_r.start()

    barrier = pltpu.get_barrier_semaphore()
    friends = [{"op": peer_of(j)} for j in range(1, chips)] + [{"op": partner}, {"sec": after}, {"sec": before}]
    for friend in friends:
        pl.semaphore_signal(barrier, inc=1, device_id=friend, device_id_type=MESH)
    pl.semaphore_wait(barrier, len(friends))

    def remote(src, dst, send, recv, device):
        copy = pltpu.make_async_remote_copy(
            src_ref=src, dst_ref=dst, send_sem=send, recv_sem=recv, device_id=device, device_id_type=MESH
        )
        return copy

    half_s, half_r = sdev // 2, rows // 2
    relayed = chips == 4
    order = [1, 2, 3] if relayed else list(range(1, chips))
    sent = []

    def go(copy):
        copy.start()
        sent.append(copy)
        return copy

    def part(r):
        return pl.ds(r * half_s, half_s)

    gathers, shares = {}, {}
    for r in (0, 1):
        shares[0, r] = go(remote(
            psi_ref.at[part(r)], got.at[me, part(r)], fwd_send.at[0, r], fwd_recv.at[0, r], {"op": partner}
        ))
    for r in (0, 1):
        for j in reversed(order):
            gathers[j, r] = go(remote(
                psi_ref.at[part(r)], got.at[me, part(r)], ag_send.at[j, r], ag_recv.at[j, r], {"op": peer_of(j)}
            ))

    def mask_in(d, r):
        row = d * rows + lax.broadcasted_iota(jnp.int32, (rows, width), 0)
        col = lax.broadcasted_iota(jnp.int32, (rows, width), 1)
        for s in range(r * half_s, (r + 1) * half_s):
            inside = (row < dims_ref[s]) & (col < dims_ref[s])
            masked[s, pl.ds(pl.multiple_of(d * rows, rows), rows), :] = jnp.where(
                inside, got[d, s], jnp.zeros((), got.dtype)
            )

    def gather(r):
        for j in order:
            gathers[j, r].wait_recv()
            slab = got.at[peer_of(j), part(r)]
            shares[j, r] = go(remote(slab, slab, fwd_send.at[j, r], fwd_recv.at[j, r], {"op": partner}))
        for j in [0] + order:
            mask_in(peer_of(j), r)
        for j in [0] + order:
            shares[j, r].wait_recv()
            mask_in(flip(chip, j, chips) * 2 + 1 - core, r)

    def terms_of(j, s):
        first = pl.multiple_of(flip(chip, j, chips) * (2 * rows), 2 * rows)
        lhs = left_v[:, s, pl.ds(first, 2 * rows), :].reshape(kdev * 2 * rows, width)
        half = jnp.dot(lhs, masked[s], preferred_element_type=jnp.float32).astype(jnp.bfloat16)
        return [lax.dot_general(
            half[k * 2 * rows:(k + 1) * 2 * rows], right_v[k, s],
            (((1,), (1,)), ((), ())), preferred_element_type=jnp.float32,
        ) for k in range(kdev)]

    chunks = list(reversed(order)) + [0]
    loads[0].wait()
    load_conn.wait()
    load_dims.wait()
    gather(0)
    load_l.wait()
    load_r.wait()
    for j in chunks[:1]:
        for s in range(half_s):
            for k, value in enumerate(terms_of(j, s)):
                begun[j, k, s] = value
    gather(1)

    weights = {}
    for k in range(kdev):
        for s in range(sdev):
            away = (conn_ref[k, s] // sdev != sec).astype(jnp.int32)
            slot = conn_ref[k, s] % sdev
            for g in range(2):
                for t in range(sdev):
                    hit = ((slot == t) & (away == 1 - g)).astype(jnp.float32)
                    weights[k, s, g, t] = hit

    core_copies = {}

    def compute(j):
        terms = {}
        for s in range(sdev):
            if s < half_s and j in chunks[:1]:
                values = [begun[j, k, s] for k in range(kdev)]
            else:
                values = terms_of(j, s)
            for k in range(kdev):
                terms[k, s] = values[k]
        theirs = pl.multiple_of((1 - core) * rows, rows)
        for g in range(2):
            for t in range(sdev):
                total = sum(weights[k, s, g, t] * terms[k, s] for k in range(kdev) for s in range(sdev))
                keep[j, g, t] = total
                give[j, g, t] = total.astype(jnp.bfloat16)
            core_copies[j, g] = go(remote(
                give.at[j, g, :, pl.ds(theirs, rows), :], from_core.at[j, g],
                core_send.at[j, g], core_recv.at[j, g], {"op": partner},
            ))

    group_of, slots_of, via_neighbour = (0, 1, 1), (1, 1, 0), (1,)

    def pair_sum(j, g, r_slot, r=None):
        start, count = (0, rows) if r is None else (r * half_r, half_r)
        mine = pl.multiple_of(core * rows + start, half_r)
        slots = slice(r_slot * half_s, (r_slot + 1) * half_s)
        return keep[j, g, slots, pl.ds(mine, count), :] + from_core[
            j, g, slots, start:start + count, :
        ].astype(jnp.float32)

    ahead, chip_copies = {}, {}

    def send_ahead(j):
        core_copies[j, 0].wait_recv()
        early[j] = pair_sum(j, 0, 0).astype(jnp.bfloat16)
        ahead[j] = go(remote(early.at[j], arrived.at[j], ahead_send.at[j], ahead_recv.at[j], {"sec": after}))

    def is_relay(j, p):
        return relayed and p in via_neighbour and j == 3

    def needs_relay(j, p, r):
        return relayed and p in via_neighbour and (j, r) in ((1, 1), (2, 0))

    def send_piece(j, p, r):
        value = pair_sum(j, group_of[p], slots_of[p], r)
        rs = slice(r * half_r, (r + 1) * half_r)
        if p == 2:
            value = value + arrived[j, :, rs, :].astype(jnp.float32)
        if needs_relay(j, p, r):
            chip_copies[3, p, r].wait_recv()
            value = value + from_chip[3, p, :, rs, :].astype(jnp.float32)
        sums[j, p, :, rs, :] = value.astype(jnp.bfloat16)
        via = (1 if r == 0 else 2) if is_relay(j, p) else j
        chip_copies[j, p, r] = go(remote(
            sums.at[j, p, :, rs, :], from_chip.at[j, p, :, rs, :],
            chip_send.at[j, p, r], chip_recv.at[j, p, r], {"op": peer_of(via)},
        ))

    def send_now(j, p):
        for r in (0, 1):
            if not needs_relay(j, p, r):
                send_piece(j, p, r)

    def relays(p):
        if relayed and p in via_neighbour:
            send_piece(1, p, 1)
            send_piece(2, p, 0)

    def own_now(j):
        core_copies[j, 1].wait_recv()
        send_now(j, 1)

    for i, j in enumerate(chunks):
        compute(j)
        if i >= 1:
            send_ahead(chunks[i - 1])
            send_now(chunks[i - 1], 0)
        if i >= 2:
            own_now(chunks[i - 2])
    if order:
        own_now(chunks[-2])
        ahead[chunks[0]].wait_recv()
        send_now(chunks[0], 2)
    send_ahead(0)
    core_copies[0, 1].wait_recv()
    relays(1)

    def sources(p):
        return order[:2] if relayed and p in via_neighbour else order

    def collect(p):
        total = pair_sum(0, group_of[p], slots_of[p])
        for j in sources(p):
            for r in (0, 1):
                chip_copies[j, p, r].wait_recv()
            total = total + from_chip[j, p].astype(jnp.float32)
        return total

    for j in chunks[1:-1]:
        ahead[j].wait_recv()
        send_now(j, 2)
    relays(2)
    onward[...] = collect(0).astype(jnp.bfloat16)
    shift = go(remote(onward, behind, z_send.at[0], z_recv.at[0], {"sec": after}))

    def put(slot, value):
        row = me * rows + lax.broadcasted_iota(jnp.int32, (rows, width), 0)
        col = lax.broadcasted_iota(jnp.int32, (rows, width), 1)
        for i in range(half_s):
            s = slot * half_s + i
            inside = (row < dims_ref[s]) & (col < dims_ref[s])
            out_ref[s] = jnp.where(inside, value[i], jnp.zeros_like(value[i])).astype(out_ref.dtype)

    own = collect(1)
    ahead[0].wait_recv()
    put(0, collect(2) + arrived[0].astype(jnp.float32))
    shift.wait_recv()
    put(1, own + behind[...].astype(jnp.float32))

    for copy in sent:
        copy.wait_send()


def on_device(n_op, n_sec, psi, left_ops, right_ops, conn, dims):
    sdev, rows, width = psi.shape
    kdev = left_ops.shape[0]
    chips, half = n_op // 2, sdev // 2
    bf16, f32 = jnp.bfloat16, jnp.float32
    dma = pltpu.SemaphoreType.DMA
    hbm = pl.BlockSpec(memory_space=pl.ANY)
    return pl.pallas_call(
        functools.partial(kernel, n_op, n_sec),
        out_shape=jax.ShapeDtypeStruct(psi.shape, psi.dtype),
        in_specs=[hbm] * 5,
        out_specs=pl.BlockSpec(memory_space=pltpu.VMEM),
        scratch_shapes=[
            pltpu.SMEM(conn.shape, conn.dtype),
            pltpu.SMEM(dims.shape, dims.dtype),
            pltpu.VMEM(left_ops.shape, bf16),
            pltpu.VMEM(right_ops.shape, bf16),
            pltpu.VMEM((n_op, sdev, rows, width), bf16),
            pltpu.VMEM((sdev, width, width), bf16),
            pltpu.VMEM((chips, kdev, half, 2 * rows, width), f32),
            pltpu.VMEM((chips, 2, sdev, 2 * rows, width), f32),
            pltpu.VMEM((chips, 2, sdev, 2 * rows, width), bf16),
            pltpu.VMEM((chips, 2, sdev, rows, width), bf16),
            pltpu.VMEM((chips, half, rows, width), bf16),
            pltpu.VMEM((chips, half, rows, width), bf16),
            pltpu.VMEM((chips, 3, half, rows, width), bf16),
            pltpu.VMEM((chips, 3, half, rows, width), bf16),
            pltpu.VMEM((half, rows, width), bf16),
            pltpu.VMEM((half, rows, width), bf16),
            dma((4,)),
            dma((1,)),
            dma((chips, 2)), dma((chips, 2)),
            dma((chips, 2)), dma((chips, 2)),
            dma((chips, 2)), dma((chips, 2)),
            dma((chips,)), dma((chips,)),
            dma((chips, 3, 2)), dma((chips, 3, 2)),
            dma((1,)), dma((1,)),
        ],
        compiler_params=pltpu.CompilerParams(
            collective_id=0, has_side_effects=True, vmem_limit_bytes=60 * 1024 * 1024
        ),
    )(conn, dims, psi, left_ops, right_ops)


def solution(mesh):
    return jax.shard_map(
        functools.partial(on_device, mesh.shape["op"], mesh.shape["sec"]),
        mesh=mesh,
        in_specs=(
            P("sec", "op", None),
            P("op", "sec", None, None),
            P("op", "sec", None, None),
            P("op", "sec"),
            P("sec"),
        ),
        out_specs=P("sec", "op", None),
        check_vma=False,
    )
```
